32 devices in a mesh: gx: 2 (over y), gy: 4 (over x, core), gz: 4 (over z).
Axes of the slice: x: 2, y: 2, z: 4, core: 2. Of those that a mesh axis runs over, the one named last changes fastest.
Arguments:
- latent: float32 [32, 64, 2048], P('gx', 'gy', 'gz'), may hold values from -6 to 6
- conv_first: bfloat16 [3, 3, 192, 64], replicated, may hold values from -0.15625 to 0.15625
- conv_second: bfloat16 [3, 3, 192, 64], replicated, may hold values from -0.15625 to 0.15625
- time_weight: float32 [64, 64], replicated, may hold values from -0.75 to 0.75
- timesteps: int32 [4], replicated, may hold values from 1 to 999
- offsets: int32 [4, 3], replicated, may hold values from 0 to 1, as said below
Outputs:
- denoised: float32 [32, 64, 2048], P('gx', 'gy', 'gz')
The draws below stay inside these ranges and needn't reach their ends.
Inputs may be any that keep to these rules, and one draw needn't show every extreme that they name: `offsets`: every entry is 0 or 1, and each of the three columns holds at least one 0 and at least one 1.
All inputs are finite; a program needn't handle non-finite values.
Results may differ from the reference program's by a relative error of at most 0.0055.
Values sent between devices are 32-bit elements; how exact they have to be, the bound alone decides.
No kernel may reach another device: no remote copies, remote signals or barrier semaphores. Data moves between devices by JAX's collectives and lax.ppermute only.
A program may use at most 64 MiB of HBM per device.

```python
import math
import jax
import jax.numpy as jnp
from jax import lax

C = 64
CX = 16
CY = 16
CZ = 8
STEPS = 4
NX = 32
NY = 64
NZ = 32
N_GX = 2
N_GY = 4
N_GZ = 4


def draw_offsets(key, part):
    columns = []
    for axis_number in range(3):
        subkey = jax.random.fold_in(key, 17 + axis_number)
        first_key, second_key = jax.random.split(subkey)
        extra = jax.random.randint(first_key, (STEPS - 2,), 0, 2).astype(jnp.int32)
        base = jnp.concatenate([jnp.array([0, 1], dtype=jnp.int32), extra])
        columns.append(jax.random.permutation(second_key, base))
    return jnp.stack(columns, axis=1).astype(jnp.int32)


def set_ends(result, key, least, high):
    longest = result.shape.index(max(result.shape))
    spots = []
    for shift in (0, 1):
        where = [jax.random.randint(jax.random.fold_in(key, axis), (), 0, length) for axis, length in enumerate(result.shape)]
        where[longest] = (where[longest] + shift) % result.shape[longest]
        spots.append(tuple(where))
    return result.at[spots[0]].set(least).at[spots[1]].set(high)


def block_scale(stream_key, dims, shards, least, top_value):
    def one(axis_at, blocks):
        draws = jax.random.uniform(jax.random.fold_in(jax.random.fold_in(stream_key, 6), axis_at), (blocks,), jnp.float32, least / len(shards), top_value / len(shards))
        return jnp.repeat(jnp.exp(draws), dims[axis_at] // blocks).reshape((-1,) + (1,) * (len(dims) - axis_at - 1))

    level = one(*shards[0])
    for cut in shards[1:]:
        level = level * one(*cut)
    return level


def gaussian(stream_key, shape, spread, bound, cuts=(), kind=jnp.bfloat16):
    values = spread * jax.random.normal(stream_key, shape, jnp.float32)
    if cuts:
        values = values * block_scale(stream_key, shape, cuts, -0.22, 0.18)
    return jnp.clip(values, -bound, bound).astype(kind)


def setup_inputs(seed: int = 0) -> dict:
    arg_keys = jax.random.split(jax.random.key(seed), 7)
    latent = gaussian(arg_keys[0], (NX, NY, NZ * C), 1.0, 6.0, ((0, 2), (1, 4), (2, 4)), jnp.float32)
    conv_first = gaussian(arg_keys[1], (3, 3, 3 * C, C), (27 * C) ** -0.5, 0.15625)
    conv_second = gaussian(arg_keys[2], (3, 3, 3 * C, C), (27 * C) ** -0.5, 0.15625)
    time_weight = gaussian(arg_keys[3], (C, C), C ** -0.5, 0.75, (), jnp.float32)
    timesteps = set_ends(jax.random.randint(arg_keys[4], (STEPS,), 1, 1000), jax.random.fold_in(arg_keys[4], 1), 1, 999).astype(jnp.int32)
    offsets = draw_offsets(jax.random.fold_in(arg_keys[6], 71), 0)
    return {"latent": latent, "conv_first": conv_first, "conv_second": conv_second, "time_weight": time_weight, "timesteps": timesteps, "offsets": offsets}


def time_bias(step_time, time_weight):
    half_c = C // 2
    freqs = jnp.exp(-math.log(10000.0) * jnp.arange(half_c, dtype=jnp.float32) / half_c)
    angles = step_time.astype(jnp.float32) * freqs
    emb = jnp.concatenate([jnp.sin(angles), jnp.cos(angles)])
    return jnp.dot(emb, time_weight, precision=lax.Precision.HIGHEST)


def to_windows(grid):
    parts = grid.reshape(N_GX, CX, N_GY, CY, N_GZ, CZ, C)
    parts = parts.transpose(0, 2, 4, 1, 3, 5, 6)
    return parts.reshape(N_GX * N_GY * N_GZ, CX, CY, CZ, C)


def from_windows(windows):
    parts = windows.reshape(N_GX, N_GY, N_GZ, CX, CY, CZ, C)
    parts = parts.transpose(0, 3, 1, 4, 2, 5, 6)
    return parts.reshape(NX, NY, NZ, C)


def window_conv(values, weight):
    kernel = weight.astype(jnp.float32).reshape(3, 3, 3, C, C)
    return lax.conv_general_dilated(values, kernel, (1, 1, 1), "SAME", dimension_numbers=("NDHWC", "DHWIO", "NDHWC"), precision=lax.Precision.HIGHEST)


def reference(latent, conv_first, conv_second, time_weight, timesteps, offsets):
    grid = latent.reshape(NX, NY, NZ, C)
    for step in range(STEPS):
        move_x = offsets[step, 0] * (CX // 2)
        move_y = offsets[step, 1] * (CY // 2)
        move_z = offsets[step, 2] * (CZ // 2)
        shifted = jnp.roll(grid, -move_x, axis=0)
        shifted = jnp.roll(shifted, -move_y, axis=1)
        shifted = jnp.roll(shifted, -move_z, axis=2)
        windows = to_windows(shifted)
        inputs = lax.optimization_barrier(windows.astype(jnp.bfloat16)).astype(jnp.float32)
        bias = time_bias(timesteps[step], time_weight)
        hidden = jax.nn.silu(window_conv(inputs, conv_first) + bias)
        hidden = lax.optimization_barrier(hidden.astype(jnp.bfloat16)).astype(jnp.float32)
        noise = window_conv(hidden, conv_second)
        if step + 1 < STEPS:
            next_time = timesteps[step + 1]
        else:
            next_time = jnp.zeros((), jnp.int32)
        delta = (next_time - timesteps[step]).astype(jnp.float32) / 1000.0
        updated = from_windows(windows + delta * noise)
        updated = jnp.roll(updated, move_z, axis=2)
        updated = jnp.roll(updated, move_y, axis=1)
        grid = jnp.roll(updated, move_x, axis=0)
    return grid.reshape(NX, NY, NZ * C)
```

```python
import math

import jax
import jax.numpy as jnp
from jax import lax
from jax.experimental import pallas as pl
from jax.experimental.pallas import tpu as pltpu
from jax.sharding import PartitionSpec as P

SPAN = 4


def passed_along(value, axis, by):
    size = lax.axis_size(axis)
    return lax.ppermute(value, axis, [(i, (i + by) % size) for i in range(size)])


def time_biases(timesteps, time_weight):
    half_c = time_weight.shape[0] // 2
    freqs = jnp.exp(-math.log(10000.0) * jnp.arange(half_c, dtype=jnp.float32) / half_c)
    angles = timesteps.astype(jnp.float32)[:, None] * freqs[None, :]
    emb = jnp.concatenate([jnp.sin(angles), jnp.cos(angles)], axis=1)
    return jnp.dot(emb, time_weight, precision=lax.Precision.HIGHEST)


def banded(weight):
    taps_x, taps_y, depth, channels = weight.shape
    step = depth // 3
    columns = [
        jnp.pad(weight, ((0, 0), (0, 0), (j * step, (SPAN - 1 - j) * step), (0, 0))) for j in range(SPAN)
    ]
    return jnp.concatenate(columns, axis=3).reshape(taps_x * taps_y * (SPAN + 2) * step, SPAN * channels)


def step_kernel(cut_ref, delta_ref, block_ref, halo_ref, first_ref, second_ref, bias_ref, out_ref, in_ref, hid_ref):
    size_x, size_y, width = block_ref.shape
    band = first_ref.shape[1]
    channels = band // SPAN
    depth = band + 2 * channels
    groups = width // band
    half = size_x // 2
    cut = cut_ref[0]
    is_cut = cut == 1

    def spread(values):
        count = values.shape[0]
        edge = jnp.zeros((count, size_y, channels), jnp.float32)
        padded = jnp.concatenate([edge, values, edge], axis=2)
        row = lax.broadcasted_iota(jnp.int32, padded.shape, 1)
        before = jnp.where(row == 0, 0.0, pltpu.roll(padded, 1, 1))
        after = jnp.where(row == size_y - 1, 0.0, pltpu.roll(padded, size_y - 1, 1))
        return [v.astype(jnp.bfloat16) for v in (before, padded, after)]

    def put(ref, start, values):
        for tap, piece in enumerate(spread(values)):
            ref[tap, pl.ds(start, values.shape[0])] = piece

    def convolve(ref, start, count, weight_ref, group):
        total = None
        lanes = pl.ds(group * band, depth)
        for tap_x in range(3):
            for tap_y in range(3):
                rows = ref[tap_y, pl.ds(start + tap_x, count), :, lanes].reshape(count * size_y, depth)
                tap = tap_x * 3 + tap_y
                part = jnp.dot(rows, weight_ref[pl.ds(tap * depth, depth), :], preferred_element_type=jnp.float32)
                total = part if total is None else total + part
        return total

    blank = jnp.zeros((3, 1, size_y, width + 2 * channels), jnp.bfloat16)
    in_ref[:, pl.ds(half + 2, 1)] = blank
    put(in_ref, 0, jnp.where(is_cut, halo_ref[pl.ds(0, 2)], 0.0))
    put(in_ref, 2, block_ref[pl.ds(0, half)])
    put(in_ref, half + 2 + cut, block_ref[pl.ds(half, half)])
    put(in_ref, size_x + 2 + cut, jnp.where(is_cut, halo_ref[pl.ds(2, 2)], 0.0))

    hid_ref[:, pl.ds(half + 1, 1)] = blank
    for side in range(2):
        start = 0 if side == 0 else half + 1 + cut
        pieces = []
        for group in range(groups):
            value = convolve(in_ref, start, half + 1, first_ref, group) + bias_ref[...]
            pieces.append(value / (1.0 + jnp.exp(-value)))
        hidden = jnp.concatenate(pieces, axis=1).reshape(half + 1, size_y, width)
        plane = lax.broadcasted_iota(jnp.int32, hidden.shape, 0)
        hidden = jnp.where((plane != (0 if side == 0 else half)) | is_cut, hidden, 0.0)
        put(hid_ref, start, hidden)

    for side in range(2):
        start = 0 if side == 0 else half + cut
        for group in range(groups):
            noise = convolve(hid_ref, start, half, second_ref, group).reshape(half, size_y, band)
            where = (pl.ds(side * half, half), slice(None), pl.ds(group * band, band))
            out_ref[where] = block_ref[where] + delta_ref[0] * noise


def denoise(block, halo, cut, delta, first, second, bias):
    size_x, size_y, width = block.shape
    channels = bias.shape[1] // SPAN
    smem = pl.BlockSpec(memory_space=pltpu.SMEM)
    vmem = pl.BlockSpec(memory_space=pltpu.VMEM)
    return pl.pallas_call(
        step_kernel,
        out_shape=jax.ShapeDtypeStruct(block.shape, jnp.float32),
        in_specs=[smem, smem, vmem, vmem, vmem, vmem, vmem],
        out_specs=vmem,
        scratch_shapes=[
            pltpu.VMEM((3, size_x + 5, size_y, width + 2 * channels), jnp.bfloat16),
            pltpu.VMEM((3, size_x + 3, size_y, width + 2 * channels), jnp.bfloat16),
        ],
        compiler_params=pltpu.CompilerParams(vmem_limit_bytes=32 << 20),
        name="denoise",
    )(cut, delta, block, halo, first, second, bias)


def slide(block, move, axis_name, axis):
    half = block.shape[axis] // 2
    lower = lax.slice_in_dim(block, 0, half, axis=axis)
    upper = lax.slice_in_dim(block, half, 2 * half, axis=axis)
    if move < 0:
        return jnp.concatenate([passed_along(upper, axis_name, 1), lower], axis)
    return jnp.concatenate([upper, passed_along(lower, axis_name, -1)], axis)


def fetch_halo(block):
    length = block.shape[0]
    size = lax.axis_size("gx")
    if size == 2:
        ends = jnp.concatenate([block[length - 2 :], block[:2]], 0)
        return passed_along(ends, "gx", 1)
    return jnp.concatenate([passed_along(block[length - 2 :], "gx", 1), passed_along(block[:2], "gx", -1)], 0)


def exchange(block, move_y, move_z, cut):
    def branch(y, z, x):
        def run(values):
            if z:
                values = slide(values, z, "gz", 2)
            if y:
                values = slide(values, y, "gy", 1)
            if x is None:
                return values
            halo = fetch_halo(values) if x else jnp.zeros((4,) + values.shape[1:], jnp.float32)
            return values, halo

        return run

    moves = (-1, 0, 1)
    if cut is None:
        branches = [branch(y, z, None) for y in moves for z in moves]
        return lax.switch((move_y + 1) * 3 + move_z + 1, branches, block)
    branches = [branch(y, z, x) for y in moves for z in moves for x in (0, 1)]
    return lax.switch(((move_y + 1) * 3 + move_z + 1) * 2 + cut, branches, block)


def shards(latent, conv_first, conv_second, time_weight, timesteps, offsets):
    count = timesteps.shape[0]
    first, second = banded(conv_first), banded(conv_second)
    bias = jnp.tile(time_biases(timesteps, time_weight), (1, SPAN))
    later = jnp.concatenate([timesteps[1:], jnp.zeros((1,), jnp.int32)])
    deltas = (later - timesteps).astype(jnp.float32) / 1000.0
    edge = jnp.zeros((1, 3), jnp.int32)
    moves = jnp.concatenate([offsets, edge]) - jnp.concatenate([edge, offsets])
    block = latent
    for step in range(count):
        cut = offsets[step, 0]
        block, halo = exchange(block, moves[step, 1], moves[step, 2], cut)
        block = denoise(
            block, halo, cut[None], deltas[step : step + 1], first, second, bias[step : step + 1]
        )
    return exchange(block, moves[count, 1], moves[count, 2], None)


def solution(mesh):
    return jax.shard_map(
        shards,
        mesh=mesh,
        in_specs=(P("gx", "gy", "gz"), P(), P(), P(), P(), P()),
        out_specs=P("gx", "gy", "gz"),
        check_vma=False,
    )
```

```python
import functools
import math

import jax
import jax.numpy as jnp
from jax import lax
from jax.experimental import pallas as pl
from jax.experimental.pallas import tpu as pltpu
from jax.sharding import PartitionSpec as P

SPAN = 4


def passed_along(value, axis, by):
    size = lax.axis_size(axis)
    return lax.ppermute(value, axis, [(i, (i + by) % size) for i in range(size)])


def prepare_kernel(
    offsets_hbm, timesteps_hbm, first_hbm, second_hbm, time_hbm, latent_hbm,
    *refs,
):
    count = timesteps_hbm.shape[0]
    pick_refs, cut_refs, delta_refs = refs[: count + 1], refs[count + 1 : 2 * count + 1], refs[2 * count + 1 : 3 * count + 1]
    bias_ref, block_ref, first_out, second_out = refs[3 * count + 1 : 3 * count + 5]
    offsets, timesteps, first, second, time_weight, sems = refs[3 * count + 5 :]

    copies = [
        pltpu.make_async_copy(source, target, sems.at[i])
        for i, (source, target) in enumerate(
            (
                (offsets_hbm, offsets),
                (timesteps_hbm, timesteps),
                (first_hbm, first),
                (second_hbm, second),
                (time_hbm, time_weight),
                (latent_hbm, block_ref),
            )
        )
    ]
    for copy in copies:
        copy.start()

    def build(source, target):
        channels, depth = source.shape[2:]
        for tap in range(9):
            taps = source[tap // 3, tap % 3].astype(jnp.float32)
            taps = jnp.concatenate([taps, jnp.zeros_like(taps)], axis=0).T
            moved = pltpu.roll(taps, channels, 1)
            edge = jnp.zeros((channels, 2 * channels), jnp.float32)
            pair = jnp.concatenate([taps, edge], axis=0) + jnp.concatenate([edge, moved], axis=0)
            rows = 4 * channels
            target[pl.ds(tap * rows, rows), :] = pair.astype(jnp.bfloat16)

    for i, (source, out) in enumerate(((first, first_out), (second, second_out))):
        copies[2 + i].wait()
        build(source, out)

    copies[0].wait()
    copies[1].wait()
    before = [0, 0, 0]
    for step in range(count + 1):
        now = [offsets[step, axis] for axis in range(3)] if step < count else [0, 0, 0]
        pick = (now[1] - before[1] + 1) * 3 + now[2] - before[2] + 1
        pick_refs[step][0] = pick * 2 + now[0] if step < count else pick
        before = now
        if step < count:
            cut_refs[step][0] = now[0]
            later = timesteps[step + 1] if step + 1 < count else 0
            delta_refs[step][0] = (later - timesteps[step]).astype(jnp.float32) / 1000.0

    copies[4].wait()
    channels = time_weight.shape[0]
    half_c = channels // 2
    shape = (bias_ref.shape[0], channels)
    place = lax.broadcasted_iota(jnp.int32, shape, 1)
    line = lax.broadcasted_iota(jnp.int32, shape, 0)
    which = jnp.where(place < half_c, place, place - half_c).astype(jnp.float32)
    time = jnp.zeros(shape, jnp.float32)
    for step in range(count):
        time = jnp.where(line == step, timesteps[step].astype(jnp.float32), time)
    angles = time * jnp.exp(-math.log(10000.0) * which / half_c)
    emb = jnp.where(place < half_c, jnp.sin(angles), jnp.cos(angles))
    bias = jnp.dot(emb, time_weight[...], precision=lax.Precision.HIGHEST, preferred_element_type=jnp.float32)
    bias_ref[...] = jnp.concatenate([bias] * SPAN, axis=1)
    copies[5].wait()


def prepare(latent, conv_first, conv_second, time_weight, timesteps, offsets):
    count = timesteps.shape[0]
    depth, channels = conv_first.shape[2:]
    first, second = conv_first.transpose(0, 1, 3, 2), conv_second.transpose(0, 1, 3, 2)
    smem = pl.BlockSpec(memory_space=pltpu.SMEM)
    vmem = pl.BlockSpec(memory_space=pltpu.VMEM)
    hbm = pl.BlockSpec(memory_space=pltpu.HBM)
    matrix = (9 * 4 * (depth // 3), 2 * channels)
    ints = lambda n: jax.ShapeDtypeStruct((n,), jnp.int32)
    real = jax.ShapeDtypeStruct((1,), jnp.float32)
    outs = pl.pallas_call(
        prepare_kernel,
        out_shape=[ints(1)] * (count + 1)
        + [ints(1)] * count
        + [real] * count
        + [jax.ShapeDtypeStruct((-(-count // 8) * 8, SPAN * channels), jnp.float32)]
        + [jax.ShapeDtypeStruct(latent.shape, latent.dtype)]
        + [jax.ShapeDtypeStruct(matrix, jnp.bfloat16)] * 2,
        in_specs=[hbm] * 6,
        out_specs=[smem] * (3 * count + 1) + [vmem] * 4,
        scratch_shapes=[
            pltpu.SMEM(offsets.shape, jnp.int32),
            pltpu.SMEM(timesteps.shape, jnp.int32),
            pltpu.VMEM(first.shape, first.dtype),
            pltpu.VMEM(second.shape, second.dtype),
            pltpu.VMEM(time_weight.shape, jnp.float32),
            pltpu.SemaphoreType.DMA((6,)),
        ],
        compiler_params=pltpu.CompilerParams(vmem_limit_bytes=12 << 20),
        name="prepare",
    )(*(pltpu.with_memory_space_constraint(a, pltpu.HBM) for a in (offsets, timesteps, first, second, time_weight, latent)))
    scalars = 3 * count + 1
    return outs[: count + 1], outs[count + 1 : 2 * count + 1], outs[2 * count + 1 : scalars], outs[scalars:]


def step_kernel(
    step, cut_ref, delta_ref, block_ref, bias_ref, first_ref, second_ref, out_ref, in_ref, hid_ref
):
    size_x, size_y, width = out_ref.shape
    band = bias_ref.shape[1]
    channels = band // SPAN
    depth = band + 2 * channels
    groups = width // band
    half = size_x // 2
    cut = cut_ref[0]
    is_cut = cut == 1

    def spread(values):
        count = values.shape[0]
        edge = jnp.zeros((count, size_y, channels), jnp.float32)
        padded = jnp.concatenate([edge, values, edge], axis=2)
        row = lax.broadcasted_iota(jnp.int32, padded.shape, 1)
        before = jnp.where(row == 0, 0.0, pltpu.roll(padded, 1, 1))
        after = jnp.where(row == size_y - 1, 0.0, pltpu.roll(padded, size_y - 1, 1))
        return [v.astype(jnp.bfloat16) for v in (before, padded, after)]

    def put(ref, start, values):
        for tap, piece in enumerate(spread(values)):
            ref[tap, pl.ds(start, values.shape[0])] = piece

    def widened(ref):
        rows = 4 * channels
        blank = jnp.zeros((2 * channels, 2 * channels), jnp.bfloat16)
        parts = []
        for tap in range(9):
            upper, lower = ref[pl.ds(tap * rows, rows // 2), :], ref[pl.ds(tap * rows + rows // 2, rows // 2), :]
            parts += [
                jnp.concatenate([upper, blank], axis=1),
                jnp.concatenate([lower, upper], axis=1),
                jnp.concatenate([blank, lower], axis=1),
            ]
        return jnp.concatenate(parts, axis=0)

    def convolve(ref, start, count, weight_ref, group):
        rows = []
        for tap in range(9):
            piece = ref[tap % 3, pl.ds(start + tap // 3, count), :, pl.ds(group * band, depth)]
            rows.append(piece.reshape(count * size_y, depth))
        return jnp.dot(jnp.concatenate(rows, axis=1), widened(weight_ref), preferred_element_type=jnp.float32)

    blank = jnp.zeros((3, 1, size_y, width + 2 * channels), jnp.bfloat16)
    in_ref[:, pl.ds(half + 2, 1)] = blank
    put(in_ref, 0, jnp.where(is_cut, block_ref[pl.ds(size_x, 2)], 0.0))
    put(in_ref, 2, block_ref[pl.ds(0, half)])
    put(in_ref, half + 2 + cut, block_ref[pl.ds(half, half)])
    put(in_ref, size_x + 2 + cut, jnp.where(is_cut, block_ref[pl.ds(size_x + 2, 2)], 0.0))

    hid_ref[:, pl.ds(half + 1, 1)] = blank
    bias = bias_ref[pl.ds(step, 1)]
    for side in range(2):
        start = 0 if side == 0 else half + 1 + cut
        pieces = []
        for group in range(groups):
            value = convolve(in_ref, start, half + 1, first_ref, group) + bias
            pieces.append(value / (1.0 + jnp.exp(-value)))
        hidden = jnp.concatenate(pieces, axis=1).reshape(half + 1, size_y, width)
        plane = lax.broadcasted_iota(jnp.int32, hidden.shape, 0)
        hidden = jnp.where((plane != (0 if side == 0 else half)) | is_cut, hidden, 0.0)
        put(hid_ref, start, hidden)

    for side in range(2):
        start = 0 if side == 0 else half + cut
        for group in range(groups):
            noise = convolve(hid_ref, start, half, second_ref, group).reshape(half, size_y, band)
            where = (pl.ds(side * half, half), slice(None), pl.ds(group * band, band))
            out_ref[where] = block_ref[where] + delta_ref[0] * noise


def denoise(step, cut, delta, block, bias, first, second):
    size_x, size_y, width = block.shape
    size_x -= 4
    channels = bias.shape[1] // SPAN
    smem = pl.BlockSpec(memory_space=pltpu.SMEM)
    vmem = pl.BlockSpec(memory_space=pltpu.VMEM)
    return pl.pallas_call(
        functools.partial(step_kernel, step),
        out_shape=jax.ShapeDtypeStruct((size_x, size_y, width), jnp.float32),
        in_specs=[smem, smem, vmem, vmem, vmem, vmem],
        out_specs=vmem,
        scratch_shapes=[
            pltpu.VMEM((3, size_x + 5, size_y, width + 2 * channels), jnp.bfloat16),
            pltpu.VMEM((3, size_x + 3, size_y, width + 2 * channels), jnp.bfloat16),
        ],
        compiler_params=pltpu.CompilerParams(vmem_limit_bytes=12 << 20),
        cost_estimate=pl.CostEstimate(flops=8000000000, bytes_accessed=60000000, transcendentals=0),
        name="denoise",
    )(cut, delta, pltpu.with_memory_space_constraint(block, pltpu.VMEM), bias, *(pltpu.with_memory_space_constraint(a, pltpu.VMEM) for a in (first, second)))


def slide(block, move, axis_name, axis):
    half = block.shape[axis] // 2
    lower = lax.slice_in_dim(block, 0, half, axis=axis)
    upper = lax.slice_in_dim(block, half, 2 * half, axis=axis)
    if move < 0:
        return jnp.concatenate([passed_along(upper, axis_name, 1), lower], axis)
    return jnp.concatenate([upper, passed_along(lower, axis_name, -1)], axis)


def fetch_halo(block):
    length = block.shape[0]
    size = lax.axis_size("gx")
    if size == 2:
        ends = jnp.concatenate([block[length - 2 :], block[:2]], 0)
        return passed_along(ends, "gx", 1)
    return jnp.concatenate([passed_along(block[length - 2 :], "gx", 1), passed_along(block[:2], "gx", -1)], 0)


def choose(index, branches, value):
    traced = jax.make_jaxpr(lambda i, v: lax.switch(i, branches, v))(index, value)
    (call,) = [e for e in traced.jaxpr.eqns if e.primitive is lax.cond_p]
    assert len(call.invars) == 2 and not traced.consts
    outs = lax.cond_p.bind(index, value, **call.params)
    return outs[0] if len(outs) == 1 else outs


def exchange(block, pick, last):
    def branch(y, z, x):
        def run(values):
            if z:
                values = slide(values, z, "gz", 2)
            if y:
                values = slide(values, y, "gy", 1)
            if x is None:
                return values
            halo = fetch_halo(values) if x else jnp.zeros((4,) + values.shape[1:], jnp.float32)
            return jnp.concatenate([values, halo], 0)

        return run

    moves = (-1, 0, 1)
    ends = (None,) if last else (0, 1)
    branches = [branch(y, z, x) for y in moves for z in moves for x in ends]
    return choose(pick.reshape(()), branches, block)


def shards(latent, conv_first, conv_second, time_weight, timesteps, offsets):
    count = timesteps.shape[0]
    picks, cuts, deltas, rest = prepare(latent, conv_first, conv_second, time_weight, timesteps, offsets)
    bias, block, first, second = rest
    for step in range(count):
        block = exchange(block, picks[step], False)
        block = denoise(step, cuts[step], deltas[step], block, bias, first, second)
    return exchange(block, picks[count], True)


def solution(mesh):
    return jax.shard_map(
        shards,
        mesh=mesh,
        in_specs=(P("gx", "gy", "gz"), P(), P(), P(), P(), P()),
        out_specs=P("gx", "gy", "gz"),
        check_vma=False,
    )
```

```python
import functools
import itertools
import math

import jax
import jax.numpy as jnp
from jax import lax
from jax.experimental import pallas as pl
from jax.experimental.pallas import tpu as pltpu
from jax.sharding import PartitionSpec as P

SPAN = 4


def passed_along(value, by):
    by = {axis: by[axis] for axis in ("gx", "gy", "gz") if by.get(axis)}
    if not by:
        return value
    names = tuple(by)
    sizes = [lax.axis_size(name) for name in names]
    pairs = []
    for place in itertools.product(*(range(size) for size in sizes)):
        target = [(at + by[name]) % size for at, name, size in zip(place, names, sizes)]
        pairs.append((flat(place, sizes), flat(target, sizes)))
    return lax.ppermute(value, names, pairs)


def flat(place, sizes):
    index = 0
    for at, size in zip(place, sizes):
        index = index * size + at
    return index


def span_of_moves(step, count):
    least = 0 if step == 0 else -1
    return least, 3 if 0 < step < count else 2


def prepare_kernel(
    offsets_hbm, timesteps_hbm, first_hbm, second_hbm, time_hbm, latent_hbm,
    *refs,
):
    count = timesteps_hbm.shape[0]
    pick_refs, cut_refs, delta_refs = refs[: count + 1], refs[count + 1 : 2 * count + 1], refs[2 * count + 1 : 3 * count + 1]
    bias_ref, block_ref, first_out, second_out = refs[3 * count + 1 : 3 * count + 5]
    offsets, timesteps, first, second, time_weight, sems = refs[3 * count + 5 :]

    copies = [
        pltpu.make_async_copy(source, target, sems.at[i])
        for i, (source, target) in enumerate(
            (
                (offsets_hbm, offsets),
                (timesteps_hbm, timesteps),
                (first_hbm, first),
                (second_hbm, second),
                (time_hbm, time_weight),
                (latent_hbm, block_ref),
            )
        )
    ]
    for copy in copies:
        copy.start()

    def build(source, target):
        channels, depth = source.shape[2:]
        for tap in range(9):
            taps = source[tap // 3, tap % 3].astype(jnp.float32)
            taps = jnp.concatenate([taps, jnp.zeros_like(taps)], axis=0).T
            moved = pltpu.roll(taps, channels, 1)
            edge = jnp.zeros((channels, 2 * channels), jnp.float32)
            pair = jnp.concatenate([taps, edge], axis=0) + jnp.concatenate([edge, moved], axis=0)
            rows = 4 * channels
            target[pl.ds(tap * rows, rows), :] = pair.astype(jnp.bfloat16)

    for i, (source, out) in enumerate(((first, first_out), (second, second_out))):
        copies[2 + i].wait()
        build(source, out)

    copies[0].wait()
    copies[1].wait()
    before = [0, 0, 0]
    for step in range(count + 1):
        now = [offsets[step, axis] for axis in range(3)] if step < count else [0, 0, 0]
        least, ways = span_of_moves(step, count)
        pick = (now[1] - before[1] - least) * ways + now[2] - before[2] - least
        pick_refs[step][0] = pick * 2 + now[0] if step < count else pick
        before = now
        if step < count:
            cut_refs[step][0] = now[0]
            later = timesteps[step + 1] if step + 1 < count else 0
            delta_refs[step][0] = (later - timesteps[step]).astype(jnp.float32) / 1000.0

    copies[4].wait()
    channels = time_weight.shape[0]
    half_c = channels // 2
    shape = (bias_ref.shape[0], channels)
    place = lax.broadcasted_iota(jnp.int32, shape, 1)
    line = lax.broadcasted_iota(jnp.int32, shape, 0)
    which = jnp.where(place < half_c, place, place - half_c).astype(jnp.float32)
    time = jnp.zeros(shape, jnp.float32)
    for step in range(count):
        time = jnp.where(line == step, timesteps[step].astype(jnp.float32), time)
    angles = time * jnp.exp(-math.log(10000.0) * which / half_c)
    emb = jnp.where(place < half_c, jnp.sin(angles), jnp.cos(angles))
    bias = jnp.dot(emb, time_weight[...], precision=lax.Precision.HIGHEST, preferred_element_type=jnp.float32)
    bias_ref[...] = jnp.concatenate([bias] * SPAN, axis=1)
    copies[5].wait()


def prepare(latent, conv_first, conv_second, time_weight, timesteps, offsets):
    count = timesteps.shape[0]
    depth, channels = conv_first.shape[2:]
    first, second = conv_first.transpose(0, 1, 3, 2), conv_second.transpose(0, 1, 3, 2)
    smem = pl.BlockSpec(memory_space=pltpu.SMEM)
    vmem = pl.BlockSpec(memory_space=pltpu.VMEM)
    hbm = pl.BlockSpec(memory_space=pltpu.HBM)
    matrix = (9 * 4 * (depth // 3), 2 * channels)
    ints = lambda n: jax.ShapeDtypeStruct((n,), jnp.int32)
    real = jax.ShapeDtypeStruct((1,), jnp.float32)
    outs = pl.pallas_call(
        prepare_kernel,
        out_shape=[ints(1)] * (count + 1)
        + [ints(1)] * count
        + [real] * count
        + [jax.ShapeDtypeStruct((-(-count // 8) * 8, SPAN * channels), jnp.float32)]
        + [jax.ShapeDtypeStruct(latent.shape, latent.dtype)]
        + [jax.ShapeDtypeStruct(matrix, jnp.bfloat16)] * 2,
        in_specs=[hbm] * 6,
        out_specs=[smem] * (3 * count + 1) + [vmem] * 4,
        scratch_shapes=[
            pltpu.SMEM(offsets.shape, jnp.int32),
            pltpu.SMEM(timesteps.shape, jnp.int32),
            pltpu.VMEM(first.shape, first.dtype),
            pltpu.VMEM(second.shape, second.dtype),
            pltpu.VMEM(time_weight.shape, jnp.float32),
            pltpu.SemaphoreType.DMA((6,)),
        ],
        compiler_params=pltpu.CompilerParams(vmem_limit_bytes=12 << 20),
        name="prepare",
    )(*(pltpu.with_memory_space_constraint(a, pltpu.HBM) for a in (offsets, timesteps, first, second, time_weight, latent)))
    scalars = 3 * count + 1
    return outs[: count + 1], outs[count + 1 : 2 * count + 1], outs[2 * count + 1 : scalars], outs[scalars:]


def step_kernel(
    step, cut_ref, delta_ref, block_ref, bias_ref, first_ref, second_ref, out_ref, in_ref, hid_ref
):
    size_x, size_y, width = out_ref.shape
    band = bias_ref.shape[1]
    channels = band // SPAN
    depth = band + 2 * channels
    groups = width // band
    half = size_x // 2
    cut = cut_ref[0]
    is_cut = cut == 1

    def spread(values):
        count = values.shape[0]
        edge = jnp.zeros((count, size_y, channels), jnp.float32)
        padded = jnp.concatenate([edge, values, edge], axis=2)
        row = lax.broadcasted_iota(jnp.int32, padded.shape, 1)
        before = jnp.where(row == 0, 0.0, pltpu.roll(padded, 1, 1))
        after = jnp.where(row == size_y - 1, 0.0, pltpu.roll(padded, size_y - 1, 1))
        return [v.astype(jnp.bfloat16) for v in (before, padded, after)]

    def put(ref, start, values):
        for tap, piece in enumerate(spread(values)):
            ref[tap, pl.ds(start, values.shape[0])] = piece

    def widened(ref):
        rows = 4 * channels
        blank = jnp.zeros((2 * channels, 2 * channels), jnp.bfloat16)
        parts = []
        for tap in range(9):
            upper, lower = ref[pl.ds(tap * rows, rows // 2), :], ref[pl.ds(tap * rows + rows // 2, rows // 2), :]
            parts += [
                jnp.concatenate([upper, blank], axis=1),
                jnp.concatenate([lower, upper], axis=1),
                jnp.concatenate([blank, lower], axis=1),
            ]
        return jnp.concatenate(parts, axis=0)

    def convolve(ref, start, count, weight_ref, group):
        rows = []
        for tap in range(9):
            piece = ref[tap % 3, pl.ds(start + tap // 3, count), :, pl.ds(group * band, depth)]
            rows.append(piece.reshape(count * size_y, depth))
        return jnp.dot(jnp.concatenate(rows, axis=1), widened(weight_ref), preferred_element_type=jnp.float32)

    blank = jnp.zeros((3, 1, size_y, width + 2 * channels), jnp.bfloat16)
    in_ref[:, pl.ds(half + 2, 1)] = blank
    put(in_ref, 0, jnp.where(is_cut, block_ref[pl.ds(size_x, 2)], 0.0))
    put(in_ref, 2, block_ref[pl.ds(0, half)])
    put(in_ref, half + 2 + cut, block_ref[pl.ds(half, half)])
    put(in_ref, size_x + 2 + cut, jnp.where(is_cut, block_ref[pl.ds(size_x + 2, 2)], 0.0))

    hid_ref[:, pl.ds(half + 1, 1)] = blank
    bias = bias_ref[pl.ds(step, 1)]
    for side in range(2):
        start = 0 if side == 0 else half + 1 + cut
        pieces = []
        for group in range(groups):
            value = convolve(in_ref, start, half + 1, first_ref, group) + bias
            pieces.append(value / (1.0 + jnp.exp(-value)))
        hidden = jnp.concatenate(pieces, axis=1).reshape(half + 1, size_y, width)
        plane = lax.broadcasted_iota(jnp.int32, hidden.shape, 0)
        hidden = jnp.where((plane != (0 if side == 0 else half)) | is_cut, hidden, 0.0)
        put(hid_ref, start, hidden)

    for side in range(2):
        start = 0 if side == 0 else half + cut
        for group in range(groups):
            noise = convolve(hid_ref, start, half, second_ref, group).reshape(half, size_y, band)
            where = (pl.ds(side * half, half), slice(None), pl.ds(group * band, band))
            out_ref[where] = block_ref[where] + delta_ref[0] * noise


def denoise(step, cut, delta, block, bias, first, second):
    size_x, size_y, width = block.shape
    size_x -= 4
    channels = bias.shape[1] // SPAN
    smem = pl.BlockSpec(memory_space=pltpu.SMEM)
    vmem = pl.BlockSpec(memory_space=pltpu.VMEM)
    return pl.pallas_call(
        functools.partial(step_kernel, step),
        out_shape=jax.ShapeDtypeStruct((size_x, size_y, width), jnp.float32),
        in_specs=[smem, smem, vmem, vmem, vmem, vmem],
        out_specs=vmem,
        scratch_shapes=[
            pltpu.VMEM((3, size_x + 5, size_y, width + 2 * channels), jnp.bfloat16),
            pltpu.VMEM((3, size_x + 3, size_y, width + 2 * channels), jnp.bfloat16),
        ],
        compiler_params=pltpu.CompilerParams(vmem_limit_bytes=12 << 20),
        cost_estimate=pl.CostEstimate(flops=8000000000, bytes_accessed=60000000, transcendentals=0),
        name="denoise",
    )(cut, delta, pltpu.with_memory_space_constraint(block, pltpu.VMEM), bias, *(pltpu.with_memory_space_constraint(a, pltpu.VMEM) for a in (first, second)))


def halves(values, move, axis):
    if move == 0:
        return [(0, values)]
    half = values.shape[axis] // 2
    lower = lax.slice_in_dim(values, 0, half, axis=axis)
    upper = lax.slice_in_dim(values, half, 2 * half, axis=axis)
    return [(1, upper), (0, lower)] if move < 0 else [(0, upper), (-1, lower)]


def slide(block, move_y, move_z):
    rows = []
    for by_y, part in halves(block, move_y, 1):
        rows.append([passed_along(piece, {"gz": by_z, "gy": by_y}) for by_z, piece in halves(part, move_z, 2)])
    return jnp.concatenate([jnp.concatenate(row, 2) for row in rows], 1)


def fetch_halo(block, move_y, move_z):
    length = block.shape[0]
    ends = [jnp.concatenate([block[length - 2 :], block[:2]], 0)]
    sides = [1]
    if lax.axis_size("gx") != 2:
        ends, sides = [block[length - 2 :], block[:2]], [1, -1]
    halos = []
    for end, by_x in zip(ends, sides):
        rows = []
        for by_y, part in halves(end, move_y, 1):
            pieces = halves(part, move_z, 2)
            rows.append([passed_along(piece, {"gz": by_z, "gy": by_y, "gx": by_x}) for by_z, piece in pieces])
        halos.append(jnp.concatenate([jnp.concatenate(row, 2) for row in rows], 1))
    return jnp.concatenate(halos, 0)


def choose(index, branches, value):
    traced = jax.make_jaxpr(lambda i, v: lax.switch(i, branches, v))(index, value)
    (call,) = [e for e in traced.jaxpr.eqns if e.primitive is lax.cond_p]
    assert len(call.invars) == 2 and not traced.consts
    outs = lax.cond_p.bind(index, value, **call.params)
    return outs[0] if len(outs) == 1 else outs


def exchange(block, pick, step, count):
    def branch(y, z, x):
        def run(values):
            moved = slide(values, y, z)
            if x is None:
                return moved
            if not x:
                halo = jnp.zeros((4,) + values.shape[1:], jnp.float32)
            elif y and z:
                halo = fetch_halo(moved, 0, 0)
            else:
                halo = fetch_halo(values, y, z)
            return jnp.concatenate([moved, halo], 0)

        return run

    least, ways = span_of_moves(step, count)
    moves = range(least, least + ways)
    ends = (0, 1) if step < count else (None,)
    branches = [branch(y, z, x) for y in moves for z in moves for x in ends]
    return choose(pick.reshape(()), branches, block)


def shards(latent, conv_first, conv_second, time_weight, timesteps, offsets):
    count = timesteps.shape[0]
    picks, cuts, deltas, rest = prepare(latent, conv_first, conv_second, time_weight, timesteps, offsets)
    bias, block, first, second = rest
    for step in range(count):
        block = exchange(block, picks[step], step, count)
        block = denoise(step, cuts[step], deltas[step], block, bias, first, second)
    return exchange(block, picks[count], count, count)


def solution(mesh):
    return jax.shard_map(
        shards,
        mesh=mesh,
        in_specs=(P("gx", "gy", "gz"), P(), P(), P(), P(), P()),
        out_specs=P("gx", "gy", "gz"),
        check_vma=False,
    )
```

```python
import functools
import itertools
import math

import jax
import jax.numpy as jnp
from jax import lax
from jax.experimental import pallas as pl
from jax.experimental.pallas import tpu as pltpu
from jax.sharding import PartitionSpec as P

PICKS, CUT = 0, 1
PICK_BITS = 5
SPAN = 4


def passed_along(value, by):
    by = {axis: by[axis] for axis in ("gx", "gy", "gz") if by.get(axis)}
    if not by:
        return value
    names = tuple(by)
    sizes = [lax.axis_size(name) for name in names]
    pairs = []
    for place in itertools.product(*(range(size) for size in sizes)):
        target = [(at + by[name]) % size for at, name, size in zip(place, names, sizes)]
        pairs.append((flat(place, sizes), flat(target, sizes)))
    return lax.ppermute(value, names, pairs)


def flat(place, sizes):
    index = 0
    for at, size in zip(place, sizes):
        index = index * size + at
    return index


def span_of_moves(step, count):
    least = 0 if step == 0 else -1
    return least, 3 if 0 < step < count else 2


def prepare_kernel(
    offsets_hbm, timesteps_hbm, first_hbm, second_hbm, time_hbm, latent_hbm,
    *refs,
):
    count = timesteps_hbm.shape[0]
    table_ref, bias_ref, block_ref, first_out, second_out = refs[:5]
    offsets, timesteps, first, second, time_weight, sems = refs[5:]

    copies = [
        pltpu.make_async_copy(source, target, sems.at[i])
        for i, (source, target) in enumerate(
            (
                (offsets_hbm, offsets),
                (timesteps_hbm, timesteps),
                (first_hbm, first),
                (second_hbm, second),
                (time_hbm, time_weight),
                (latent_hbm, block_ref),
            )
        )
    ]
    for copy in copies:
        copy.start()

    def build(source, target):
        channels, depth = source.shape[2:]
        for tap in range(9):
            taps = source[tap // 3, tap % 3].astype(jnp.float32)
            taps = jnp.concatenate([taps, jnp.zeros_like(taps)], axis=0).T
            moved = pltpu.roll(taps, channels, 1)
            edge = jnp.zeros((channels, 2 * channels), jnp.float32)
            pair = jnp.concatenate([taps, edge], axis=0) + jnp.concatenate([edge, moved], axis=0)
            rows = 4 * channels
            target[pl.ds(tap * rows, rows), :] = pair.astype(jnp.bfloat16)

    for i, (source, out) in enumerate(((first, first_out), (second, second_out))):
        copies[2 + i].wait()
        build(source, out)

    copies[0].wait()
    copies[1].wait()
    before = [0, 0, 0]
    line = lax.broadcasted_iota(jnp.int32, table_ref.shape, 0)
    place = lax.broadcasted_iota(jnp.int32, table_ref.shape, 1)
    table = jnp.zeros(table_ref.shape, jnp.int32)
    picks = 1
    for step in range(count + 1):
        now = [offsets[step, axis] for axis in range(3)] if step < count else [0, 0, 0]
        least, ways = span_of_moves(step, count)
        pick = (now[1] - before[1] - least) * ways + now[2] - before[2] - least
        pick = pick * 2 + now[0] if step < count else pick
        picks = picks + (pick << (PICK_BITS * step))
        table = jnp.where(line == step, now[0], table)
        before = now
    table_ref[...] = jnp.where(place == PICKS, picks, table)

    copies[4].wait()
    channels = time_weight.shape[0]
    half_c = channels // 2
    shape = (bias_ref.shape[1], channels)
    place = lax.broadcasted_iota(jnp.int32, shape, 1)
    line = lax.broadcasted_iota(jnp.int32, shape, 0)
    which = jnp.where(place < half_c, place, place - half_c).astype(jnp.float32)
    time, delta = jnp.zeros(shape, jnp.float32), jnp.zeros(shape, jnp.float32)
    for step in range(count):
        later = timesteps[step + 1] if step + 1 < count else 0
        time = jnp.where(line == step, timesteps[step].astype(jnp.float32), time)
        delta = jnp.where(line == step, (later - timesteps[step]).astype(jnp.float32), delta)
    angles = time * jnp.exp(-math.log(10000.0) * which / half_c)
    emb = jnp.where(place < half_c, jnp.sin(angles), jnp.cos(angles))
    bias = jnp.dot(emb, time_weight[...], precision=lax.Precision.HIGHEST, preferred_element_type=jnp.float32)
    bias_ref[0] = jnp.concatenate([bias] * SPAN, axis=1)
    bias_ref[1] = jnp.concatenate([delta / 1000.0] * SPAN, axis=1)
    copies[5].wait()


def prepare(latent, conv_first, conv_second, time_weight, timesteps, offsets):
    count = timesteps.shape[0]
    depth, channels = conv_first.shape[2:]
    first, second = conv_first.transpose(0, 1, 3, 2), conv_second.transpose(0, 1, 3, 2)
    vmem = pl.BlockSpec(memory_space=pltpu.VMEM)
    hbm = pl.BlockSpec(memory_space=pltpu.HBM)
    matrix = (9 * 4 * (depth // 3), 2 * channels)
    lines = -(-(count + 1) // 8) * 8
    return pl.pallas_call(
        prepare_kernel,
        out_shape=[
            jax.ShapeDtypeStruct((lines, 128), jnp.int32),
            jax.ShapeDtypeStruct((2, lines, SPAN * channels), jnp.float32),
            jax.ShapeDtypeStruct(latent.shape, latent.dtype),
            jax.ShapeDtypeStruct(matrix, jnp.bfloat16),
            jax.ShapeDtypeStruct(matrix, jnp.bfloat16),
        ],
        in_specs=[hbm] * 6,
        out_specs=[vmem] * 5,
        scratch_shapes=[
            pltpu.SMEM(offsets.shape, jnp.int32),
            pltpu.SMEM(timesteps.shape, jnp.int32),
            pltpu.VMEM(first.shape, first.dtype),
            pltpu.VMEM(second.shape, second.dtype),
            pltpu.VMEM(time_weight.shape, jnp.float32),
            pltpu.SemaphoreType.DMA((6,)),
        ],
        compiler_params=pltpu.CompilerParams(vmem_limit_bytes=12 << 20),
        name="prepare",
    )(*(pltpu.with_memory_space_constraint(a, pltpu.HBM) for a in (offsets, timesteps, first, second, time_weight, latent)))


def step_kernel(
    step, table_ref, block_ref, bias_ref, first_ref, second_ref, out_ref, in_ref, hid_ref
):
    size_x, size_y, width = out_ref.shape
    band = bias_ref.shape[2]
    channels = band // SPAN
    depth = band + 2 * channels
    groups = width // band
    half = size_x // 2
    cut = table_ref[step, CUT]
    is_cut = cut == 1

    def spread(values):
        count = values.shape[0]
        edge = jnp.zeros((count, size_y, channels), jnp.float32)
        padded = jnp.concatenate([edge, values, edge], axis=2)
        row = lax.broadcasted_iota(jnp.int32, padded.shape, 1)
        before = jnp.where(row == 0, 0.0, pltpu.roll(padded, 1, 1))
        after = jnp.where(row == size_y - 1, 0.0, pltpu.roll(padded, size_y - 1, 1))
        return [v.astype(jnp.bfloat16) for v in (before, padded, after)]

    def put(ref, start, values):
        for tap, piece in enumerate(spread(values)):
            ref[tap, pl.ds(start, values.shape[0])] = piece

    def widened(ref):
        rows = 4 * channels
        blank = jnp.zeros((2 * channels, 2 * channels), jnp.bfloat16)
        parts = []
        for tap in range(9):
            upper, lower = ref[pl.ds(tap * rows, rows // 2), :], ref[pl.ds(tap * rows + rows // 2, rows // 2), :]
            parts += [
                jnp.concatenate([upper, blank], axis=1),
                jnp.concatenate([lower, upper], axis=1),
                jnp.concatenate([blank, lower], axis=1),
            ]
        return jnp.concatenate(parts, axis=0)

    def convolve(ref, start, count, weight_ref, group):
        rows = []
        for tap in range(9):
            piece = ref[tap % 3, pl.ds(start + tap // 3, count), :, pl.ds(group * band, depth)]
            rows.append(piece.reshape(count * size_y, depth))
        return jnp.dot(jnp.concatenate(rows, axis=1), widened(weight_ref), preferred_element_type=jnp.float32)

    blank = jnp.zeros((3, 1, size_y, width + 2 * channels), jnp.bfloat16)
    in_ref[:, pl.ds(half + 2, 1)] = blank
    put(in_ref, 0, jnp.where(is_cut, block_ref[pl.ds(size_x, 2)], 0.0))
    put(in_ref, 2, block_ref[pl.ds(0, half)])
    put(in_ref, half + 2 + cut, block_ref[pl.ds(half, half)])
    put(in_ref, size_x + 2 + cut, jnp.where(is_cut, block_ref[pl.ds(size_x + 2, 2)], 0.0))

    hid_ref[:, pl.ds(half + 1, 1)] = blank
    bias = bias_ref[0, pl.ds(step, 1)]
    for side in range(2):
        start = 0 if side == 0 else half + 1 + cut
        pieces = []
        for group in range(groups):
            value = convolve(in_ref, start, half + 1, first_ref, group) + bias
            pieces.append(value / (1.0 + jnp.exp(-value)))
        hidden = jnp.concatenate(pieces, axis=1).reshape(half + 1, size_y, width)
        plane = lax.broadcasted_iota(jnp.int32, hidden.shape, 0)
        hidden = jnp.where((plane != (0 if side == 0 else half)) | is_cut, hidden, 0.0)
        put(hid_ref, start, hidden)

    delta = bias_ref[1, pl.ds(step, 1)]
    for side in range(2):
        start = 0 if side == 0 else half + cut
        for group in range(groups):
            noise = (delta * convolve(hid_ref, start, half, second_ref, group)).reshape(half, size_y, band)
            where = (pl.ds(side * half, half), slice(None), pl.ds(group * band, band))
            out_ref[where] = block_ref[where] + noise


def denoise(step, table, block, bias, first, second):
    size_x, size_y, width = block.shape
    size_x -= 4
    channels = bias.shape[2] // SPAN
    vmem = pl.BlockSpec(memory_space=pltpu.VMEM)
    return pl.pallas_call(
        functools.partial(step_kernel, step),
        out_shape=jax.ShapeDtypeStruct((size_x, size_y, width), jnp.float32),
        in_specs=[vmem] * 5,
        out_specs=vmem,
        scratch_shapes=[
            pltpu.VMEM((3, size_x + 5, size_y, width + 2 * channels), jnp.bfloat16),
            pltpu.VMEM((3, size_x + 3, size_y, width + 2 * channels), jnp.bfloat16),
        ],
        compiler_params=pltpu.CompilerParams(vmem_limit_bytes=12 << 20),
        cost_estimate=pl.CostEstimate(flops=8000000000, bytes_accessed=60000000, transcendentals=0),
        name="denoise",
    )(table, pltpu.with_memory_space_constraint(block, pltpu.VMEM), bias, *(pltpu.with_memory_space_constraint(a, pltpu.VMEM) for a in (first, second)))


def halves(values, move, axis):
    if move == 0:
        return [(0, values)]
    half = values.shape[axis] // 2
    lower = lax.slice_in_dim(values, 0, half, axis=axis)
    upper = lax.slice_in_dim(values, half, 2 * half, axis=axis)
    return [(1, upper), (0, lower)] if move < 0 else [(0, upper), (-1, lower)]


def slide(block, move_y, move_z):
    rows = []
    for by_y, part in halves(block, move_y, 1):
        rows.append([passed_along(piece, {"gz": by_z, "gy": by_y}) for by_z, piece in halves(part, move_z, 2)])
    return jnp.concatenate([jnp.concatenate(row, 2) for row in rows], 1)


def fetch_halo(block, move_y, move_z):
    length = block.shape[0]
    ends = [jnp.concatenate([block[length - 2 :], block[:2]], 0)]
    sides = [1]
    if lax.axis_size("gx") != 2:
        ends, sides = [block[length - 2 :], block[:2]], [1, -1]
    halos = []
    for end, by_x in zip(ends, sides):
        rows = []
        for by_y, part in halves(end, move_y, 1):
            pieces = halves(part, move_z, 2)
            rows.append([passed_along(piece, {"gz": by_z, "gy": by_y, "gx": by_x}) for by_z, piece in pieces])
        halos.append(jnp.concatenate([jnp.concatenate(row, 2) for row in rows], 1))
    return jnp.concatenate(halos, 0)


def choose(index, branches, value):
    traced = jax.make_jaxpr(lambda i, v: lax.switch(i, branches, v))(index, value)
    (call,) = [e for e in traced.jaxpr.eqns if e.primitive is lax.cond_p]
    assert len(call.invars) == 2 and not traced.consts
    outs = lax.cond_p.bind(index, value, **call.params)
    return outs[0] if len(outs) == 1 else outs


def exchange(block, pick, step, count):
    def branch(y, z, x):
        def run(values):
            moved = slide(values, y, z)
            if x is None:
                return moved
            if not x:
                halo = jnp.zeros((4,) + values.shape[1:], jnp.float32)
            elif y and z:
                halo = fetch_halo(moved, 0, 0)
            else:
                halo = fetch_halo(values, y, z)
            return jnp.concatenate([moved, halo], 0)

        return run

    least, ways = span_of_moves(step, count)
    moves = range(least, least + ways)
    ends = (0, 1) if step < count else (None,)
    branches = [branch(y, z, x) for y in moves for z in moves for x in ends]
    return choose(pick.reshape(()), branches, block)


def shards(latent, conv_first, conv_second, time_weight, timesteps, offsets):
    count = timesteps.shape[0]
    table, bias, block, first, second = prepare(latent, conv_first, conv_second, time_weight, timesteps, offsets)
    picks = lax.optimization_barrier(table[0, PICKS]) - 1
    for step in range(count):
        block = exchange(block, picks >> (PICK_BITS * step) & (1 << PICK_BITS) - 1, step, count)
        block = denoise(step, table, block, bias, first, second)
    return exchange(block, picks >> (PICK_BITS * count), count, count)


def solution(mesh):
    return jax.shard_map(
        shards,
        mesh=mesh,
        in_specs=(P("gx", "gy", "gz"), P(), P(), P(), P(), P()),
        out_specs=P("gx", "gy", "gz"),
        check_vma=False,
    )
```

```python
import functools
import itertools
import math

import jax
import jax.numpy as jnp
from jax import lax
from jax.experimental import pallas as pl
from jax.experimental.pallas import tpu as pltpu
from jax.sharding import PartitionSpec as P

PICKS, CUT = 0, 1
PICK_BITS = 5
SPAN = 4


def passed_along(value, by):
    by = {axis: by[axis] for axis in ("gx", "gy", "gz") if by.get(axis)}
    if not by:
        return value
    names = tuple(by)
    sizes = [lax.axis_size(name) for name in names]
    pairs = []
    for place in itertools.product(*(range(size) for size in sizes)):
        target = [(at + by[name]) % size for at, name, size in zip(place, names, sizes)]
        pairs.append((flat(place, sizes), flat(target, sizes)))
    return lax.ppermute(value, names, pairs)


def flat(place, sizes):
    index = 0
    for at, size in zip(place, sizes):
        index = index * size + at
    return index


def span_of_moves(step, count):
    least = 0 if step == 0 else -1
    return least, 3 if 0 < step < count else 2


def prepare_kernel(
    offsets_hbm, timesteps_hbm, first_hbm, second_hbm, time_hbm, latent_hbm,
    *refs,
):
    count = timesteps_hbm.shape[0]
    table_ref, bias_ref, block_ref, first_out, second_out = refs[:5]
    offsets, timesteps, first, second, time_weight, sems = refs[5:]

    copies = [
        pltpu.make_async_copy(source, target, sems.at[i])
        for i, (source, target) in enumerate(
            (
                (offsets_hbm, offsets),
                (timesteps_hbm, timesteps),
                (first_hbm, first),
                (second_hbm, second),
                (time_hbm, time_weight),
                (latent_hbm, block_ref),
            )
        )
    ]
    for copy in copies:
        copy.start()

    def build(source, target):
        channels, depth = source.shape[2:]
        for tap in range(9):
            taps = source[tap // 3, tap % 3].astype(jnp.float32)
            taps = jnp.concatenate([taps, jnp.zeros_like(taps)], axis=0).T
            moved = pltpu.roll(taps, channels, 1)
            edge = jnp.zeros((channels, 2 * channels), jnp.float32)
            pair = jnp.concatenate([taps, edge], axis=0) + jnp.concatenate([edge, moved], axis=0)
            rows = 4 * channels
            target[pl.ds(tap * rows, rows), :] = pair.astype(jnp.bfloat16)

    for i, (source, out) in enumerate(((first, first_out), (second, second_out))):
        copies[2 + i].wait()
        build(source, out)

    copies[0].wait()
    copies[1].wait()
    before = [0, 0, 0]
    line = lax.broadcasted_iota(jnp.int32, table_ref.shape, 0)
    place = lax.broadcasted_iota(jnp.int32, table_ref.shape, 1)
    table = jnp.zeros(table_ref.shape, jnp.int32)
    picks = 1
    for step in range(count + 1):
        now = [offsets[step, axis] for axis in range(3)] if step < count else [0, 0, 0]
        least, ways = span_of_moves(step, count)
        pick = (now[1] - before[1] - least) * ways + now[2] - before[2] - least
        pick = pick * 2 + now[0] if step < count else pick
        picks = picks + (pick << (PICK_BITS * step))
        table = jnp.where(line == step, now[0], table)
        before = now
    table_ref[...] = jnp.where(place == PICKS, picks, table)

    copies[4].wait()
    channels = time_weight.shape[0]
    half_c = channels // 2
    shape = (bias_ref.shape[1], channels)
    place = lax.broadcasted_iota(jnp.int32, shape, 1)
    line = lax.broadcasted_iota(jnp.int32, shape, 0)
    which = jnp.where(place < half_c, place, place - half_c).astype(jnp.float32)
    time, delta = jnp.zeros(shape, jnp.float32), jnp.zeros(shape, jnp.float32)
    for step in range(count):
        later = timesteps[step + 1] if step + 1 < count else 0
        time = jnp.where(line == step, timesteps[step].astype(jnp.float32), time)
        delta = jnp.where(line == step, (later - timesteps[step]).astype(jnp.float32), delta)
    angles = time * jnp.exp(-math.log(10000.0) * which / half_c)
    emb = jnp.where(place < half_c, jnp.sin(angles), jnp.cos(angles))
    bias = jnp.dot(emb, time_weight[...], precision=lax.Precision.HIGHEST, preferred_element_type=jnp.float32)
    bias_ref[0] = jnp.concatenate([bias] * SPAN, axis=1)
    bias_ref[1] = jnp.concatenate([delta / 1000.0] * SPAN, axis=1)
    copies[5].wait()


def prepare(latent, conv_first, conv_second, time_weight, timesteps, offsets):
    count = timesteps.shape[0]
    depth, channels = conv_first.shape[2:]
    first, second = conv_first.transpose(0, 1, 3, 2), conv_second.transpose(0, 1, 3, 2)
    vmem = pl.BlockSpec(memory_space=pltpu.VMEM)
    hbm = pl.BlockSpec(memory_space=pltpu.HBM)
    matrix = (9 * 4 * (depth // 3), 2 * channels)
    lines = -(-(count + 1) // 8) * 8
    return pl.pallas_call(
        prepare_kernel,
        out_shape=[
            jax.ShapeDtypeStruct((lines, 128), jnp.int32),
            jax.ShapeDtypeStruct((2, lines, SPAN * channels), jnp.float32),
            jax.ShapeDtypeStruct(latent.shape, latent.dtype),
            jax.ShapeDtypeStruct(matrix, jnp.bfloat16),
            jax.ShapeDtypeStruct(matrix, jnp.bfloat16),
        ],
        in_specs=[hbm] * 6,
        out_specs=[vmem] * 5,
        scratch_shapes=[
            pltpu.SMEM(offsets.shape, jnp.int32),
            pltpu.SMEM(timesteps.shape, jnp.int32),
            pltpu.VMEM(first.shape, first.dtype),
            pltpu.VMEM(second.shape, second.dtype),
            pltpu.VMEM(time_weight.shape, jnp.float32),
            pltpu.SemaphoreType.DMA((6,)),
        ],
        compiler_params=pltpu.CompilerParams(vmem_limit_bytes=12 << 20),
        name="prepare",
    )(*(pltpu.with_memory_space_constraint(a, pltpu.HBM) for a in (offsets, timesteps, first, second, time_weight, latent)))


def step_kernel(
    step, table_ref, block_ref, bias_ref, first_ref, second_ref, out_ref, in_ref, hid_ref
):
    size_x, size_y, width = out_ref.shape
    band = bias_ref.shape[2]
    channels = band // SPAN
    depth = band + 2 * channels
    groups = width // band
    half = size_x // 2
    is_cut = jnp.broadcast_to(table_ref[pl.ds(step, 1), pl.ds(CUT, 1)][None], (1, size_y, width)) == 1

    def if_cut(values):
        return jnp.where(is_cut, values, 0.0)

    def unless_cut(values):
        return jnp.where(is_cut, 0.0, values)

    def spread(values):
        count = values.shape[0]
        edge = jnp.zeros((count, size_y, channels), jnp.float32)
        padded = jnp.concatenate([edge, values, edge], axis=2)
        row = lax.broadcasted_iota(jnp.int32, padded.shape, 1)
        before = jnp.where(row == 0, 0.0, pltpu.roll(padded, 1, 1))
        after = jnp.where(row == size_y - 1, 0.0, pltpu.roll(padded, size_y - 1, 1))
        return [v.astype(jnp.bfloat16) for v in (before, padded, after)]

    def put(ref, side, start, values):
        for tap, piece in enumerate(spread(values)):
            ref[side, tap, pl.ds(start, values.shape[0])] = piece

    def widened(ref):
        rows = 4 * channels
        blank = jnp.zeros((2 * channels, 2 * channels), jnp.bfloat16)
        parts = []
        for tap in range(9):
            upper, lower = ref[pl.ds(tap * rows, rows // 2), :], ref[pl.ds(tap * rows + rows // 2, rows // 2), :]
            parts += [
                jnp.concatenate([upper, blank], axis=1),
                jnp.concatenate([lower, upper], axis=1),
                jnp.concatenate([blank, lower], axis=1),
            ]
        return jnp.concatenate(parts, axis=0)

    def convolve(ref, side, count, weight_ref, group):
        rows = []
        for tap in range(9):
            piece = ref[side, tap % 3, pl.ds(tap // 3, count), :, pl.ds(group * band, depth)]
            rows.append(piece.reshape(count * size_y, depth))
        return jnp.dot(jnp.concatenate(rows, axis=1), widened(weight_ref), preferred_element_type=jnp.float32)

    put(in_ref, 0, 0, if_cut(block_ref[pl.ds(size_x, 2)]))
    put(in_ref, 0, 2, block_ref[pl.ds(0, half)])
    put(in_ref, 0, half + 2, unless_cut(block_ref[pl.ds(half, 1)]))
    put(in_ref, 1, 0, unless_cut(block_ref[pl.ds(half - 1, 1)]))
    put(in_ref, 1, 1, block_ref[pl.ds(half, half)])
    put(in_ref, 1, half + 1, if_cut(block_ref[pl.ds(size_x + 2, 2)]))

    bias = bias_ref[0, pl.ds(step, 1)]
    for side in range(2):
        pieces = []
        for group in range(groups):
            value = convolve(in_ref, side, half + 1, first_ref, group) + bias
            pieces.append(value / (1.0 + jnp.exp(-value)))
        hidden = jnp.concatenate(pieces, axis=1).reshape(half + 1, size_y, width)
        if side == 0:
            put(hid_ref, 0, 0, if_cut(hidden[:1]))
            put(hid_ref, 0, 1, hidden[1:])
            put(hid_ref, 1, 0, unless_cut(hidden[half:]))
        else:
            put(hid_ref, 1, 1, hidden[:half])
            put(hid_ref, 1, half + 1, if_cut(hidden[half:]))
            put(hid_ref, 0, half + 1, unless_cut(hidden[:1]))

    delta = bias_ref[1, pl.ds(step, 1)]
    for side in range(2):
        for group in range(groups):
            noise = (delta * convolve(hid_ref, side, half, second_ref, group)).reshape(half, size_y, band)
            where = (pl.ds(side * half, half), slice(None), pl.ds(group * band, band))
            out_ref[where] = block_ref[where] + noise


def denoise(step, table, block, bias, first, second):
    size_x, size_y, width = block.shape
    size_x -= 4
    channels = bias.shape[2] // SPAN
    vmem = pl.BlockSpec(memory_space=pltpu.VMEM)
    return pl.pallas_call(
        functools.partial(step_kernel, step),
        out_shape=jax.ShapeDtypeStruct((size_x, size_y, width), jnp.float32),
        in_specs=[vmem] * 5,
        out_specs=vmem,
        scratch_shapes=[
            pltpu.VMEM((2, 3, size_x // 2 + 3, size_y, width + 2 * channels), jnp.bfloat16),
            pltpu.VMEM((2, 3, size_x // 2 + 2, size_y, width + 2 * channels), jnp.bfloat16),
        ],
        compiler_params=pltpu.CompilerParams(vmem_limit_bytes=12 << 20),
        cost_estimate=pl.CostEstimate(flops=8000000000, bytes_accessed=60000000, transcendentals=0),
        name="denoise",
    )(table, pltpu.with_memory_space_constraint(block, pltpu.VMEM), bias, *(pltpu.with_memory_space_constraint(a, pltpu.VMEM) for a in (first, second)))


def halves(values, move, axis):
    if move == 0:
        return [(0, values)]
    half = values.shape[axis] // 2
    lower = lax.slice_in_dim(values, 0, half, axis=axis)
    upper = lax.slice_in_dim(values, half, 2 * half, axis=axis)
    return [(1, upper), (0, lower)] if move < 0 else [(0, upper), (-1, lower)]


def slide(block, move_y, move_z):
    rows = []
    for by_y, part in halves(block, move_y, 1):
        rows.append([passed_along(piece, {"gz": by_z, "gy": by_y}) for by_z, piece in halves(part, move_z, 2)])
    return jnp.concatenate([jnp.concatenate(row, 2) for row in rows], 1)


def fetch_halo(block, move_y, move_z):
    length = block.shape[0]
    ends = [jnp.concatenate([block[length - 2 :], block[:2]], 0)]
    sides = [1]
    if lax.axis_size("gx") != 2:
        ends, sides = [block[length - 2 :], block[:2]], [1, -1]
    halos = []
    for end, by_x in zip(ends, sides):
        rows = []
        for by_y, part in halves(end, move_y, 1):
            pieces = halves(part, move_z, 2)
            rows.append([passed_along(piece, {"gz": by_z, "gy": by_y, "gx": by_x}) for by_z, piece in pieces])
        halos.append(jnp.concatenate([jnp.concatenate(row, 2) for row in rows], 1))
    return jnp.concatenate(halos, 0)


def choose(index, branches, value):
    traced = jax.make_jaxpr(lambda i, v: lax.switch(i, branches, v))(index, value)
    (call,) = [e for e in traced.jaxpr.eqns if e.primitive is lax.cond_p]
    assert len(call.invars) == 2 and not traced.consts
    outs = lax.cond_p.bind(index, value, **call.params)
    return outs[0] if len(outs) == 1 else outs


def exchange(block, pick, step, count):
    def branch(y, z, x):
        def run(values):
            moved = slide(values, y, z)
            if x is None:
                return moved
            if not x:
                halo = jnp.zeros((4,) + values.shape[1:], jnp.float32)
            elif y and z:
                halo = fetch_halo(moved, 0, 0)
            else:
                halo = fetch_halo(values, y, z)
            return jnp.concatenate([moved, halo], 0)

        return run

    least, ways = span_of_moves(step, count)
    moves = range(least, least + ways)
    ends = (0, 1) if step < count else (None,)
    branches = [branch(y, z, x) for y in moves for z in moves for x in ends]
    return choose(pick.reshape(()), branches, block)


def shards(latent, conv_first, conv_second, time_weight, timesteps, offsets):
    count = timesteps.shape[0]
    table, bias, block, first, second = prepare(latent, conv_first, conv_second, time_weight, timesteps, offsets)
    picks = lax.optimization_barrier(table[0, PICKS]) - 1
    for step in range(count):
        block = exchange(block, picks >> (PICK_BITS * step) & (1 << PICK_BITS) - 1, step, count)
        block = denoise(step, table, block, bias, first, second)
    return exchange(block, picks >> (PICK_BITS * count), count, count)


def solution(mesh):
    return jax.shard_map(
        shards,
        mesh=mesh,
        in_specs=(P("gx", "gy", "gz"), P(), P(), P(), P(), P()),
        out_specs=P("gx", "gy", "gz"),
        check_vma=False,
    )
```
